256 devices in a mesh: mod: 16 (over z, y_lo), pulse: 16 (over y_hi, x, core).
Axes of the slice: x: 4, y: 4 (y_hi: 2, y_lo: 2; y = y_hi * 2 + y_lo), z: 8, core: 2. Of those that a mesh axis runs over, the one named last changes fastest.
Arguments:
- raw_frames: bfloat16 [16, 16, 16, 128, 512], P('pulse', None, 'mod'), may hold values from -6 to 6
- gain_section: int32 [16, 16, 16, 16, 512], P('pulse', None, 'mod'), may hold values from 0 to 6560, as said below
- offset: float32 [16, 3, 128, 512], P('mod'), may hold values from -3 to 3
- gain_factor: float32 [16, 3, 128, 512], P('mod'), may hold values from 0.5 to 2
- row_map: bfloat16 [1024, 1024], replicated, as said below
- column_map: bfloat16 [1024, 1024], replicated
- reference_image: bfloat16 [1024, 1024], P(('mod', 'pulse')), may hold values from -6 to 6
- shifts: int32 [2, 16, 16, 64], P(None, 'pulse', 'mod'), may hold values from -24 to 24
Outputs:
- scores: float32 [16, 16, 64], P('pulse', 'mod')
- new_reference: float32 [1024, 1024], P(('mod', 'pulse'))
The draws below stay inside these ranges and needn't reach their ends.
Inputs may be any that keep to these rules, and one draw needn't show every extreme that they name: `gain_section`: each word holds the gain sections 0, 1 or 2 of 8 consecutive pixel rows in base 3, row 8 p + k as the digit of 3 ** k. row_map and column_map are the identity plus a dense interpolation part.
All inputs are finite; a program needn't handle non-finite values.
Results may differ from the reference program's by a relative error of at most 0.0005.
The reference program's roundings to bfloat16 on the way (of `calibrated`, `assembled`, `row_mapped` and `lab_image`) count: a program that leaves them out, or rounds other values in their place, can miss the bound.
Values may be sent and summed in bfloat16 or wider, within the bound.
A program may use at most 128 MiB of HBM per device.

```python
import math
import jax
import jax.numpy as jnp
from jax import lax

MODULES = 16
MR = 128
MC = 512
F_DEV = 16
TS = 128
SH = 24
BATCHES = 16
IMG_H = 1024
IMG_W = 1024
TILES = 64


def interpolation(key, order):
    deviation = jax.random.normal(key, (order, order), jnp.float32)
    return (jnp.eye(order, dtype=jnp.float32) + 0.5 * deviation / math.sqrt(order)).astype(jnp.bfloat16)


def draw_gain_section(key, part):
    section_codes = jax.random.randint(jax.random.fold_in(key, 7), (BATCHES, F_DEV, MODULES, MR // 8, 8, MC), 0, 3, dtype=jnp.int32)
    powers = jnp.array([1, 3, 9, 27, 81, 243, 729, 2187], dtype=jnp.int32)
    fields = section_codes * powers[:, None]
    return jnp.sum(fields, axis=4, dtype=jnp.int32)


def draw_row_map(key, part):
    return interpolation(jax.random.fold_in(key, 11), IMG_H)


def draw_column_map(key, part):
    return interpolation(jax.random.fold_in(key, 23), IMG_W)


def place_ends(entries, own_key, low, top_value):
    longest = entries.shape.index(max(entries.shape))
    spots = []
    for shift in (0, 1):
        where = [jax.random.randint(jax.random.fold_in(own_key, axis), (), 0, length) for axis, length in enumerate(entries.shape)]
        where[longest] = (where[longest] + shift) % entries.shape[longest]
        spots.append(tuple(where))
    return entries.at[spots[0]].set(low).at[spots[1]].set(top_value)


def block_scale(key, shape, cuts, low, high):
    gain, own = 1.0, jax.random.fold_in(key, 6)
    for position, shards_of in cuts:
        draws = jnp.exp(jax.random.uniform(jax.random.fold_in(own, position), (shards_of,), jnp.float32, low / len(cuts), high / len(cuts)))
        gain = gain * jnp.repeat(draws, shape[position] // shards_of).reshape([-1 if axis == position else 1 for axis in range(len(shape))])
    return gain


def centred(own_key, shape, spread, limit, split=(), kind=jnp.bfloat16):
    drawn = jax.random.normal(own_key, shape, jnp.float32) * spread
    if len(split) > 0:
        drawn = block_scale(own_key, shape, split, -0.22, 0.18) * drawn
    return jnp.clip(drawn, min=-limit, max=limit).astype(kind)


def setup_inputs(seed: int = 0) -> dict:
    streams_of = jax.random.split(jax.random.key(seed), 9)
    raw_frames = centred(streams_of[0], (BATCHES, F_DEV, MODULES, MR, MC), 1.0, 6.0, ((0, 16), (2, 16)))
    gain_section = draw_gain_section(jax.random.fold_in(streams_of[8], 71), 0)
    offset = centred(streams_of[2], (MODULES, 3, MR, MC), 0.5, 3.0, ((0, 16),), jnp.float32)
    gain_factor = jnp.clip(jnp.exp(math.log(2.0) - 1.3862944 * jax.random.uniform(streams_of[3], (MODULES, 3, MR, MC), jnp.float32) ** block_scale(streams_of[3], (MODULES, 3, MR, MC), ((0, 16),), -0.2, 0.2)), 0.5, 2.0)
    row_map = draw_row_map(jax.random.fold_in(streams_of[8], 71), 0)
    column_map = draw_column_map(jax.random.fold_in(streams_of[8], 71), 0)
    reference_image = centred(streams_of[6], (IMG_H, IMG_W), 1.0, 6.0, ((0, 256),))
    shifts = place_ends(jax.random.randint(streams_of[7], (2, BATCHES, F_DEV, TILES), 0 - SH, SH + 1), jax.random.fold_in(streams_of[7], 1), 0 - SH, SH).astype(jnp.int32)
    return {"raw_frames": raw_frames, "gain_section": gain_section, "offset": offset, "gain_factor": gain_factor, "row_map": row_map, "column_map": column_map, "reference_image": reference_image, "shifts": shifts}


prior_weight = 16.0


def unpack_section(packed):
    powers = jnp.array([1, 3, 9, 27, 81, 243, 729, 2187], dtype=jnp.int32)
    section = jnp.remainder(jnp.floor_divide(packed[..., :, None, :], powers[:, None]), 3).astype(jnp.int32)
    return section.reshape(packed.shape[:-2] + (packed.shape[-2] * 8, packed.shape[-1]))


def calibrate(raw_frames, gain_section, offset, gain_factor):
    dark_level = jnp.where(gain_section == 0, offset[:, 0], jnp.where(gain_section == 1, offset[:, 1], offset[:, 2]))
    factor = jnp.where(gain_section == 0, gain_factor[:, 0], jnp.where(gain_section == 1, gain_factor[:, 1], gain_factor[:, 2]))
    return ((raw_frames.astype(jnp.float32) - dark_level) * factor).astype(jnp.bfloat16)


def assemble(modules_now):
    quadrants = modules_now.reshape(2, 2, 4, MR, MC)
    return quadrants.transpose(0, 2, 3, 1, 4).reshape(8 * MR, 2 * MC)


def frame_image(modules_now, row_map, column_map):
    assembled = assemble(modules_now)
    row_mapped = jnp.dot(row_map, assembled, preferred_element_type=jnp.float32).astype(jnp.bfloat16)
    return jnp.dot(row_mapped, column_map, preferred_element_type=jnp.float32).astype(jnp.bfloat16)


def track_tiles(lab_image, ref_padded, shift_rows, shift_cols, splat_map, cover_map):
    tiles_across = lab_image.shape[1] // TS
    tiles_count = (lab_image.shape[0] // TS) * tiles_across

    def tile_step(index, carried):
        splat_map, cover_map, scores = carried
        index = jnp.asarray(index).astype(jnp.int32)
        row_start = (index // tiles_across) * TS
        col_start = (index % tiles_across) * TS
        top_edge = (row_start + shift_rows[index] + SH).astype(jnp.int32)
        left_edge = (col_start + shift_cols[index] + SH).astype(jnp.int32)
        frame_tile = lax.dynamic_slice(lab_image, (row_start, col_start), (TS, TS)).astype(jnp.float32)
        window = lax.dynamic_slice(ref_padded, (top_edge, left_edge), (TS, TS)).astype(jnp.float32)
        score_value = jnp.sum(frame_tile * window) / TS
        weight = jax.nn.sigmoid(score_value)
        current = lax.dynamic_slice(splat_map, (top_edge, left_edge), (TS, TS))
        splat_map = lax.dynamic_update_slice(splat_map, current + weight * frame_tile, (top_edge, left_edge))
        current = lax.dynamic_slice(cover_map, (top_edge, left_edge), (TS, TS))
        cover_map = lax.dynamic_update_slice(cover_map, current + weight, (top_edge, left_edge))
        scores = scores.at[index].set(score_value)
        return splat_map, cover_map, scores

    start = (splat_map, cover_map, jnp.zeros((tiles_count,), jnp.float32))
    return lax.fori_loop(0, tiles_count, tile_step, start)


def reference(raw_frames, gain_section, offset, gain_factor, row_map, column_map, reference_image, shifts):
    frames_total = raw_frames.shape[0] * raw_frames.shape[1]
    raw_all = raw_frames.reshape(frames_total, MODULES, MR, MC)
    gain_all = gain_section.reshape(frames_total, MODULES, MR // 8, MC)
    rows_all = shifts[0].reshape(frames_total, TILES)
    cols_all = shifts[1].reshape(frames_total, TILES)
    height = 8 * MR
    width = 2 * MC
    ref_padded = jnp.pad(reference_image, SH)
    empty = jnp.zeros((height + 2 * SH, width + 2 * SH), jnp.float32)

    def per_frame(carried, inputs):
        raw_now, gain_now, rows_now, cols_now = inputs
        calibrated = calibrate(raw_now, unpack_section(gain_now), offset, gain_factor)
        lab_image = frame_image(calibrated, row_map, column_map)
        splat_map, cover_map, scores = track_tiles(lab_image, ref_padded, rows_now, cols_now, carried[0], carried[1])
        return (splat_map, cover_map), scores

    (splat_map, cover_map), scores = lax.scan(per_frame, (empty, empty), (raw_all, gain_all, rows_all, cols_all))
    splat_map = splat_map[SH:SH + height, SH:SH + width]
    cover_map = cover_map[SH:SH + height, SH:SH + width]
    new_reference = (splat_map + prior_weight * reference_image.astype(jnp.float32)) / (cover_map + prior_weight)
    return scores.reshape(raw_frames.shape[0], raw_frames.shape[1], TILES), new_reference
```

```python
import functools

import jax
import jax.numpy as jnp
from jax import lax
from jax.experimental import pallas as pl
from jax.experimental.pallas import tpu as pltpu
from jax.sharding import PartitionSpec as P

MR = 128
MC = 512
TS = 128
SH = 24
TILES = 64
IMG = 1024
PRIOR = 16.0
MESH = pl.DeviceIdType.MESH
F32 = jnp.float32
BF16 = jnp.bfloat16
I32 = jnp.int32


def coords():
    mod = lax.axis_index("mod")
    pulse = lax.axis_index("pulse")
    z = mod // 2
    y = (pulse // 8) * 2 + mod % 2
    x = (pulse // 2) % 4
    core = pulse % 2
    return z, y, x, core


def device(z, y, x, core):
    return (z * 2 + y % 2, (y // 2) * 8 + x * 2 + core)


def remote(src, dst, send_sem, recv_sem, target):
    return pltpu.make_async_remote_copy(
        src_ref=src,
        dst_ref=dst,
        send_sem=send_sem,
        recv_sem=recv_sem,
        device_id=target,
        device_id_type=MESH,
    )


def greet(targets):
    barrier = pltpu.get_barrier_semaphore()
    for target in targets:
        pl.semaphore_signal(barrier, inc=1, device_id=target, device_id_type=MESH)
    pl.semaphore_wait(barrier, len(targets))


VM = pl.BlockSpec(memory_space=pltpu.VMEM)
ANY = pl.BlockSpec(memory_space=pl.ANY)


def calibrate_kernel(raw_ref, gain_ref, off_ref, fac_ref, out_ref):
    k = lax.broadcasted_iota(I32, (8, MC), 0)
    inv = jnp.full((8, MC), 1.0, F32)
    for step in range(1, 8):
        inv = jnp.where(k == step, jnp.float32(1.0 / 3.0**step), inv)
    inv_next = inv * jnp.float32(1.0 / 3.0)
    for p in range(MR // 8):
        rows = pl.ds(8 * p, 8)
        packed = gain_ref[0, pl.ds(p, 1), :].astype(F32) + 0.5
        packed = jnp.broadcast_to(packed, (8, MC))
        digit = jnp.floor(packed * inv) - 3.0 * jnp.floor(packed * inv_next)
        low = digit < 0.5
        mid = digit < 1.5
        dark = jnp.where(low, off_ref[0, rows, :], jnp.where(mid, off_ref[1, rows, :], off_ref[2, rows, :]))
        fac = jnp.where(low, fac_ref[0, rows, :], jnp.where(mid, fac_ref[1, rows, :], fac_ref[2, rows, :]))
        value = (raw_ref[0, rows, :].astype(F32) - dark) * fac
        out_ref[0, rows, :] = value.astype(BF16)


def calibrate(raw, gain, off, fac):
    frames = raw.shape[0]
    return pl.pallas_call(
        calibrate_kernel,
        grid=(frames,),
        in_specs=[
            pl.BlockSpec((1, MR, MC), lambda f: (f, 0, 0)),
            pl.BlockSpec((1, MR // 8, MC), lambda f: (f, 0, 0)),
            pl.BlockSpec((3, MR, MC), lambda f: (0, 0, 0)),
            pl.BlockSpec((3, MR, MC), lambda f: (0, 0, 0)),
        ],
        out_specs=pl.BlockSpec((1, MR, MC), lambda f: (f, 0, 0)),
        out_shape=jax.ShapeDtypeStruct((frames, MR, MC), BF16),
        name="calibrate",
    )(raw, gain, off, fac)


def exchange_kernel(
    cal_ref, ref_ref, sh_ref,
    img_ref, rf_ref, shc_ref, sha_ref,
    ra, rtmp, rsl, rb, rc, srow, srow_in, sx, sy,
    a_send, a_recv, r_send, r_recv, z_send, z_recv, y_send, y_recv,
    c_send, c_recv, x_send, x_recv, s_send, s_recv, l_sem,
):
    z, y, x, core = coords()
    mod = lax.axis_index("mod")
    pulse = lax.axis_index("pulse")
    peers = [((mod + i) % 16, pulse) for i in range(1, 16)]
    plane = [device(z, y, (x + (i // 2)) % 4, (core + i) % 2) for i in range(1, 8)]
    greet(peers + plane + [device(z, (y + 2) % 4, x, core), device(z, (y + 3 - 2 * (y % 2)) % 4, x, core)])

    quad = mod // 4
    row0 = pl.multiple_of((quad // 2) * 512 + (mod % 4) * MR, MR)
    col0 = pl.multiple_of((quad % 2) * MC, MC)
    spot = img_ref.at[pl.ds(row0, MR), pl.ds(col0, MC)]

    j = x * 2 + core
    first = []
    for i in range(1, 8):
        copy = remote(ref_ref, ra.at[j], r_send.at[i - 1], r_recv.at[i - 1], plane[i - 1])
        copy.start()
        first.append(copy)
    own_ref = pltpu.make_async_copy(ref_ref, ra.at[j], l_sem.at[0])
    own_ref.start()

    lane = lax.broadcasted_iota(I32, (2, 128), 1)
    srow[:, 0:64] = sh_ref[...]
    srow[:, 64:128] = sh_ref[...]
    srow[...] = jnp.where(lane // 64 == core, srow[...], 0)
    partner = device(z, y, x, 1 - core)
    s0 = remote(srow, srow_in, s_send.at[0], s_recv.at[0], partner)
    s0.start()

    big = []
    for i in range(1, 16):
        copy = remote(cal_ref.at[(mod + i) % 16], spot, a_send.at[i - 1], a_recv.at[i - 1], peers[i - 1])
        copy.start()
        big.append(copy)
    own = pltpu.make_async_copy(cal_ref.at[mod], spot, l_sem.at[1])
    own.start()

    for copy in first:
        copy.wait()
    own_ref.wait()
    mine = pl.ds(pl.multiple_of(j * 128, 128), 128)
    for i in range(8):
        rtmp[4 * i:4 * i + 4, :] = ra[i, :, mine].astype(F32)
    rsl[...] = rtmp[...].astype(BF16)

    second = []
    for i in range(1, 8):
        copy = remote(rsl, rb.at[z], z_send.at[i - 1], z_recv.at[i - 1], device((z + i) % 8, y, x, core))
        copy.start()
        second.append(copy)
    own_z = pltpu.make_async_copy(rsl, rb.at[z], l_sem.at[0])
    own_z.start()

    s0.wait()
    shc_ref[...] = srow[...] + srow_in[...]
    sx[pl.ds(x, 1)] = shc_ref[...].reshape(1, 2, 128)
    s1 = []
    for i in range(1, 4):
        copy = remote(sx.at[x], sx.at[x], s_send.at[i], s_recv.at[i], device(z, y, (x + i) % 4, core))
        copy.start()
        s1.append(copy)

    for copy in second:
        copy.wait()
    own_z.wait()
    yrow = (y % 2) * 2 + y // 2
    third = []
    for i in range(1, 4):
        copy = remote(rb, rc.at[:, yrow], y_send.at[i - 1], y_recv.at[i - 1], device(z, (y + i) % 4, x, core))
        copy.start()
        third.append(copy)
    own_y = pltpu.make_async_copy(rb, rc.at[:, yrow], l_sem.at[0])
    own_y.start()

    for copy in s1:
        copy.wait()
    s2 = []
    for i in range(1, 4):
        copy = remote(sx, sy.at[y], s_send.at[3 + i], s_recv.at[3 + i], device(z, (y + i) % 4, x, core))
        copy.start()
        s2.append(copy)
    own_s = pltpu.make_async_copy(sx, sy.at[y], l_sem.at[2])
    own_s.start()

    for copy in third:
        copy.wait()
    own_y.wait()
    fourth = remote(rc.at[pl.ds(3 * (1 - core), 5)], rf_ref.at[x, core], c_send, c_recv, partner)
    fourth.start()
    own_c = pltpu.make_async_copy(rc.at[pl.ds(3 * core, 5)], rf_ref.at[x, core], l_sem.at[0])
    own_c.start()

    for copy in s2:
        copy.wait()
    own_s.wait()
    s3 = []
    for i in range(1, 8):
        copy = remote(sy, sha_ref.at[z], s_send.at[6 + i], s_recv.at[6 + i], device((z + i) % 8, y, x, core))
        copy.start()
        s3.append(copy)
    own_s2 = pltpu.make_async_copy(sy, sha_ref.at[z], l_sem.at[2])
    own_s2.start()

    fourth.wait()
    own_c.wait()
    fifth = []
    for i in range(1, 4):
        copy = remote(rf_ref.at[x], rf_ref.at[x], x_send.at[i - 1], x_recv.at[i - 1], device(z, y, (x + i) % 4, core))
        copy.start()
        fifth.append(copy)

    for copy in s3:
        copy.wait()
    own_s2.wait()
    for copy in fifth:
        copy.wait()
    for copy in big:
        copy.wait()
    own.wait()


def exchange(cal, ref, sh):
    dma = pltpu.SemaphoreType.DMA
    return pl.pallas_call(
        exchange_kernel,
        in_specs=[ANY, VM, VM],
        out_specs=[ANY, VM, VM, VM],
        out_shape=[
            jax.ShapeDtypeStruct((IMG, IMG), BF16),
            jax.ShapeDtypeStruct((4, 2, 5, 4, 32, 128), BF16),
            jax.ShapeDtypeStruct((2, 128), I32),
            jax.ShapeDtypeStruct((8, 4, 4, 2, 128), I32),
        ],
        scratch_shapes=[
            pltpu.VMEM((8, 4, IMG), BF16),
            pltpu.VMEM((32, 128), F32),
            pltpu.VMEM((32, 128), BF16),
            pltpu.VMEM((8, 32, 128), BF16),
            pltpu.VMEM((8, 4, 32, 128), BF16),
            pltpu.VMEM((2, 128), I32),
            pltpu.VMEM((2, 128), I32),
            pltpu.VMEM((4, 2, 128), I32),
            pltpu.VMEM((4, 4, 2, 128), I32),
            dma((15,)), dma((15,)), dma((7,)), dma((7,)), dma((7,)), dma((7,)), dma((3,)), dma((3,)),
            dma(()), dma(()), dma((3,)), dma((3,)), dma((14,)), dma((14,)), dma((3,)),
        ],
        compiler_params=pltpu.CompilerParams(collective_id=0, has_side_effects=True),
        name="exchange",
    )(cal, ref, sh)


def swap_kernel(rm_ref, out_ref, send, recv, sem):
    z, y, x, core = coords()
    partner = device(z, y, x, 1 - core)
    greet([partner])
    give = pl.ds(pl.multiple_of((1 - core) * 512, 512), 512)
    keep = pl.ds(pl.multiple_of(core * 512, 512), 512)
    copy = remote(rm_ref.at[give], out_ref.at[core], send, recv, partner)
    copy.start()
    own = pltpu.make_async_copy(rm_ref.at[keep], out_ref.at[core], sem)
    own.start()
    copy.wait()
    own.wait()


def swap(rm):
    dma = pltpu.SemaphoreType.DMA
    return pl.pallas_call(
        swap_kernel,
        in_specs=[VM],
        out_specs=VM,
        out_shape=jax.ShapeDtypeStruct((2, 512, IMG), BF16),
        scratch_shapes=[dma(()), dma(()), dma(())],
        compiler_params=pltpu.CompilerParams(collective_id=1, has_side_effects=True),
        name="swap",
    )(rm)


RROWS = 704
SROWS = 576


def track_kernel(core_ref, sh_ref, lab_ref, rf_ref, main_ref, halo_ref, row_ref, r3, held, part, wts, sp):
    core = core_ref[0]
    zero = jnp.zeros((RROWS, 128), F32)
    r3[0] = zero
    r3[9] = zero
    for b in range(8):
        r3[b + 1, 0:32, :] = jnp.zeros((32, 128), F32)
        r3[b + 1, 32:672, :] = rf_ref[b // 2, b % 2].reshape(640, 128).astype(F32)
        r3[b + 1, 672:704, :] = jnp.zeros((32, 128), F32)
    for b in range(10):
        sp[b] = jnp.zeros((SROWS, 128), F32)
    lane = lax.broadcasted_iota(I32, (TS, 128), 1)

    def place(t):
        g = t // 32
        ty = (t // 8) % 4
        tx = t % 8
        col = g * 64 + core * 32 + t % 32
        dy = sh_ref[0, col]
        dx = sh_ref[1, col]
        back = jnp.where(dx < 0, 1, 0).astype(I32)
        return g, ty, tx, dy, dx + 128 * back, tx + 1 - back

    def score_step(t, carry):
        g, ty, tx, dy, turn, block = place(t)
        tile = lab_ref[g, pl.ds(pl.multiple_of(ty * TS, TS), TS), pl.ds(pl.multiple_of(tx * 128, 128), 128)]
        tile = pltpu.roll(tile.astype(F32), turn, 1)
        held[t] = tile
        top = core * 128 + 32 + ty * TS + dy
        near = r3[block, pl.ds(top, TS), :]
        far = r3[block + 1, pl.ds(top, TS), :]
        product = tile * jnp.where(lane >= turn, near, far)
        part[t] = jnp.sum(product.reshape(16, 8, 128), axis=0)
        return carry

    lax.fori_loop(0, 64, score_step, 0)
    sums = jnp.sum(part[...], axis=1)
    score = jnp.broadcast_to(jnp.sum(sums, axis=1, keepdims=True) / TS, (64, 128))
    wts[...] = 1.0 / (1.0 + jnp.exp(-score))
    t_of = lax.broadcasted_iota(I32, (64, 128), 0)
    l_of = lax.broadcasted_iota(I32, (64, 128), 1)
    hit = l_of == (t_of // 32) * 64 + core * 32 + t_of % 32
    row_ref[...] = jnp.sum(jnp.where(hit, score, 0.0), axis=0, keepdims=True)

    def splat_step(t, carry):
        g, ty, tx, dy, turn, block = place(t)
        value = held[t] * wts[pl.ds(t, 1), :]
        top = 32 + ty * TS + dy
        sp[block, pl.ds(top, TS), :] += jnp.where(lane >= turn, value, 0.0)
        sp[block + 1, pl.ds(top, TS), :] += jnp.where(lane >= turn, 0.0, value)
        return carry

    lax.fori_loop(0, 64, splat_step, 0)
    edge = pl.multiple_of((1 - core) * 544, 32)
    for b in range(8):
        main_ref[b] = sp[b + 1, 32:544, :]
        halo_ref[b] = sp[b + 1, pl.ds(edge, 32), :]


def track(core, shc, lab, rf):
    return pl.pallas_call(
        track_kernel,
        in_specs=[
            pl.BlockSpec(memory_space=pltpu.SMEM),
            pl.BlockSpec(memory_space=pltpu.SMEM),
            VM,
            VM,
        ],
        out_specs=[VM, VM, VM],
        out_shape=[
            jax.ShapeDtypeStruct((8, 512, 128), F32),
            jax.ShapeDtypeStruct((8, 32, 128), F32),
            jax.ShapeDtypeStruct((1, 128), F32),
        ],
        scratch_shapes=[
            pltpu.VMEM((10, RROWS, 128), F32),
            pltpu.VMEM((64, TS, 128), F32),
            pltpu.VMEM((64, 8, 128), F32),
            pltpu.VMEM((64, 128), F32),
            pltpu.VMEM((10, SROWS, 128), F32),
        ],
        name="track",
    )(core, shc, lab, rf)


def ring_start(piece, me, right, left, fwd_a, fwd_b, fin_l, fin_r, send, recv):
    copies = [
        remote(piece((me + 2) % 4, 0), fwd_a, send.at[0], recv.at[0], right),
        remote(piece((me + 2) % 4, 1), fwd_b, send.at[1], recv.at[1], left),
        remote(piece((me + 1) % 4, 1), fin_l.at[1], send.at[2], recv.at[2], right),
        remote(piece((me + 3) % 4, 0), fin_r.at[0], send.at[3], recv.at[3], left),
    ]
    for copy in copies:
        copy.start()
    return copies


def ring_pass(piece, me, right, left, fwd_a, fwd_b, fin_l, fin_r, sum_a, sum_b, send, recv, copies):
    copies[0].wait_recv()
    sum_a[...] = fwd_a[...] + piece((me + 1) % 4, 0)[...]
    onward_a = remote(sum_a, fin_l.at[0], send.at[4], recv.at[4], right)
    onward_a.start()
    copies[1].wait_recv()
    sum_b[...] = fwd_b[...] + piece((me + 3) % 4, 1)[...]
    onward_b = remote(sum_b, fin_r.at[1], send.at[5], recv.at[5], left)
    onward_b.start()
    return copies + [onward_a, onward_b]


def ring_end(copies):
    for n, copy in enumerate(copies):
        copy.wait_send()
        if n >= 2:
            copy.wait_recv()


def finish_kernel(
    main_ref, halo_ref, row_ref, sha_ref, ref_ref,
    out_ref, score_ref,
    acc, halo_in, row_in, wx, wy, wz, smat, dmat, wmat, lhs, cov, unit, p_fwd, p_fin, p_sum, q_fwd, q_fin, q_sum, mid_p, mid_q,
    p2_fwd, p2_fin, p2_sum, q2_fwd, q2_fin, q2_sum, zout, zin,
    h_send, h_recv, w_send, w_recv, p_send, p_recv, q_send, q_recv, p2_send, p2_recv, q2_send, q2_recv,
    z_send, z_recv, l_sem,
):
    z, y, x, core = coords()
    partner = device(z, y, x, 1 - core)
    xs = [device(z, y, (x + i) % 4, core) for i in range(1, 4)]
    ys = [device(z, (y + i) % 4, x, core) for i in range(1, 4)]
    zs = [device((z + i) % 8, y, x, core) for i in range(1, 8)]
    zo = [device((z + i) % 8, y, x, 1 - core) for i in range(1, 8)]
    greet([partner] + xs + ys + zs + zo)

    halo = remote(halo_ref, halo_in, h_send, h_recv, partner)
    halo.start()
    row = remote(row_ref, row_in, w_send.at[0], w_recv.at[0], partner)
    row.start()
    acc[...] = main_ref[...].reshape(acc.shape)
    halo.wait()
    edge = 3 - 3 * core
    yl = 1 - core
    for b in range(8):
        acc[b, edge, yl, yl] += halo_in[b].reshape(4, 8, 128)

    def piece_px(d, half):
        return acc.at[pl.ds(2 * half, 2), :, :, :, d]

    def piece_qy(d, half):
        return acc.at[pl.ds(4 + 2 * half, 2), :, d % 2, d // 2]

    xr, xl = xs[0], xs[2]
    yr, yl_dev = ys[0], ys[2]
    args_p = (piece_px, x, xr, xl, p_fwd.at[0], p_fwd.at[1], p_fin.at[0], p_fin.at[1])
    args_q = (piece_qy, y, yr, yl_dev, q_fwd.at[0], q_fwd.at[1], q_fin.at[0], q_fin.at[1])
    cp = ring_start(*args_p, p_send, p_recv)
    cq = ring_start(*args_q, q_send, q_recv)

    row.wait()
    chip = row_ref[...] + row_in[...]
    both = jnp.where(core == 0, chip[:, 0:64], chip[:, 64:128])
    score_ref[...] = both
    wx[pl.ds(x, 1)] = chip.reshape(1, 1, 128)
    w1 = []
    for i in range(3):
        copy = remote(wx.at[x], wx.at[x], w_send.at[1 + i], w_recv.at[1 + i], xs[i])
        copy.start()
        w1.append(copy)

    cp = ring_pass(*args_p, p_sum.at[0], p_sum.at[1], p_send, p_recv, cp)
    cq = ring_pass(*args_q, q_sum.at[0], q_sum.at[1], q_send, q_recv, cq)

    for copy in w1:
        copy.wait()
    w2 = []
    for i in range(3):
        copy = remote(wx, wy.at[y], w_send.at[4 + i], w_recv.at[4 + i], ys[i])
        copy.start()
        w2.append(copy)
    own_w = pltpu.make_async_copy(wx, wy.at[y], l_sem.at[0])
    own_w.start()

    gather_rows(sha_ref, 0, smat)
    gather_rows(sha_ref, 1, dmat)
    smat[...] = jnp.transpose(smat[...])
    lane = lax.broadcasted_iota(I32, (128, 128), 1)
    for k in range(3):
        ty = jnp.clip(z - 1 + k, 0, 7)
        for g in range(2):
            moved = pltpu.roll(dmat[...], (128 - (g * 64 + ty * 8)) % 128, 1)
            for tx in range(8):
                dx = jnp.broadcast_to(moved[:, tx:tx + 1], (128, 128))
                edge_hit = jnp.where(lane < 64, jnp.where(lane < dx, 1.0, 0.0), jnp.where(lane >= 128 + dx, 1.0, 0.0))
                edge_hit = jnp.where(lane == 63, 1.0, edge_hit)
                unit[tx, pl.ds((2 * k + g) * 128, 128), :] = edge_hit.astype(BF16)

    for copy in w2:
        copy.wait()
    own_w.wait()
    w3 = []
    for i in range(7):
        copy = remote(wy, wz.at[z], w_send.at[7 + i], w_recv.at[7 + i], zs[i])
        copy.start()
        w3.append(copy)
    own_w2 = pltpu.make_async_copy(wy, wz.at[z], l_sem.at[0])
    own_w2.start()

    ring_end(cp)
    for h in range(2):
        mid_p[pl.ds(2 * h, 2)] = piece_px(x, h)[...] + p_fin[0, h] + p_fin[1, h]

    def piece_py(d, half):
        return mid_p.at[pl.ds(2 * half, 2), :, d % 2, d // 2]

    args_p2 = (piece_py, y, yr, yl_dev, p2_fwd.at[0], p2_fwd.at[1], p2_fin.at[0], p2_fin.at[1])
    cp2 = ring_start(*args_p2, p2_send, p2_recv)
    ring_end(cq)
    for h in range(2):
        mid_q[pl.ds(2 * h, 2)] = piece_qy(y, h)[...] + q_fin[0, h] + q_fin[1, h]

    def piece_qx(d, half):
        return mid_q.at[pl.ds(2 * half, 2), :, d]

    args_q2 = (piece_qx, x, xr, xl, q2_fwd.at[0], q2_fwd.at[1], q2_fin.at[0], q2_fin.at[1])
    cq2 = ring_start(*args_q2, q2_send, q2_recv)
    cp2 = ring_pass(*args_p2, p2_sum.at[0], p2_sum.at[1], p2_send, p2_recv, cp2)
    cq2 = ring_pass(*args_q2, q2_sum.at[0], q2_sum.at[1], q2_send, q2_recv, cq2)
    ring_end(cp2)
    ring_end(cq2)
    for h in range(2):
        got_p = piece_py(y, h)[...] + p2_fin[0, h] + p2_fin[1, h]
        got_q = piece_qx(x, h)[...] + q2_fin[0, h] + q2_fin[1, h]
        for b in range(2):
            for d in range(4):
                zout[d, 0, 2 * h + b] = got_p[b, d, 0:4, :]
                zout[d, 1, 2 * h + b] = got_p[b, d, 4:8, :]
                zout[d, 0, 4 + 2 * h + b] = got_q[b, d, 0:4, :]
                zout[d, 1, 4 + 2 * h + b] = got_q[b, d, 4:8, :]

    for d in range(4):
        for c in range(2):
            target_z = 4 * core + d
            self_hit = jnp.logical_and(target_z == z, core == c)

            @pl.when(jnp.logical_not(self_hit))
            def _():
                remote(zout.at[d, c], zin.at[z], z_send.at[d, c], z_recv.at[z], device(target_z, y, x, c)).start()

            @pl.when(self_hit)
            def _():
                pltpu.make_async_copy(zout.at[d, c], zin.at[z], l_sem.at[1]).start()

    for copy in w3:
        copy.wait()
    own_w2.wait()
    gather_rows(wz, 0, wmat)
    wmat[...] = jnp.transpose(1.0 / (1.0 + jnp.exp(-wmat[...])))
    r0 = z * 128 + (y % 2) * 64 + (y // 2) * 32 + x * 8 + core * 4
    for k in range(3):
        ty = jnp.clip(z - 1 + k, 0, 7)
        valid = jnp.where(ty == z - 1 + k, 1.0, 0.0).astype(F32)
        for g in range(2):
            rows = pl.ds(pl.multiple_of(g * 64 + ty * 8, 8), 8)
            low = smat[rows, :] + (ty * 128).astype(F32)
            w = wmat[rows, :] * valid
            w1 = w.astype(BF16).astype(F32)
            w2 = (w - w1).astype(BF16).astype(F32)
            w3 = w - w1 - w2
            cols = slice((2 * k + g) * 128, (2 * k + g + 1) * 128)
            for i in range(4):
                r = (r0 + i).astype(F32)
                hit = jnp.logical_and(low <= r, r < low + 128.0)
                for n, part in enumerate((w1, w2, w3)):
                    lhs[n * 4 + i, :, cols] = jnp.where(hit, part, 0.0)
    left = lhs[...].reshape(96, 768).astype(BF16)
    sub = lax.broadcasted_iota(I32, (12, 8, 128), 1)
    found = jnp.zeros((12, 8, 128), F32)
    for tx in range(8):
        product = jnp.dot(left, unit[tx], preferred_element_type=F32).reshape(12, 8, 128)
        found = jnp.where(sub == tx, product, found)
    found = found[0:4] + found[4:8] + found[8:12]
    tx_of = lax.broadcasted_iota(I32, (8, 128), 0)
    l_of = lax.broadcasted_iota(I32, (8, 128), 1)
    for i in range(4):
        total = jnp.sum(jnp.where(l_of == 63, found[i], 0.0), axis=1, keepdims=True)
        side = jnp.where(l_of == 63, 0.0, found[i])
        before = jnp.where(tx_of == 0, 0.0, pltpu.roll(side, 1, 0))
        after = jnp.where(tx_of == 7, 0.0, pltpu.roll(side, 7, 0))
        cover = total - side + jnp.where(l_of < 64, before, after)
        for b in range(8):
            cov[b, i:i + 1, :] = cover[b:b + 1, :]

    for d in range(4):
        for c in range(2):
            target_z = 4 * core + d
            self_hit = jnp.logical_and(target_z == z, core == c)

            @pl.when(jnp.logical_not(self_hit))
            def _():
                remote(zout.at[d, c], zin.at[z], z_send.at[d, c], z_recv.at[z], device(target_z, y, x, c)).wait_send()

    for s in range(8):
        self_hit = jnp.logical_and(z == s, core == z // 4)

        @pl.when(jnp.logical_not(self_hit))
        def _():
            remote(zout.at[0, 0], zin.at[s], z_send.at[0, 0], z_recv.at[s], partner).wait_recv()

        @pl.when(self_hit)
        def _():
            pltpu.make_async_copy(zout.at[0, 0], zin.at[s], l_sem.at[1]).wait()

    own_ref = ref_ref[...].astype(F32)
    for b in range(8):
        total = zin[0, b]
        for s in range(1, 8):
            total = total + zin[s, b]
        cols = slice(128 * b, 128 * b + 128)
        out_ref[:, cols] = (total + PRIOR * own_ref[:, cols]) / (cov[b] + PRIOR)


def gather_rows(source, which, target):
    def step(i, carry):
        target[pl.ds(i, 1), :] = source[i // 16, (i // 4) % 4, i % 4, which:which + 1, :].astype(target.dtype)
        return carry

    lax.fori_loop(0, 128, step, 0)


def finish(main, halo, row, sha, ref):
    dma = pltpu.SemaphoreType.DMA
    vm = pltpu.VMEM
    return pl.pallas_call(
        finish_kernel,
        in_specs=[VM, VM, VM, VM, VM],
        out_specs=[VM, VM],
        out_shape=[
            jax.ShapeDtypeStruct((4, IMG), F32),
            jax.ShapeDtypeStruct((1, 64), F32),
        ],
        scratch_shapes=[
            vm((8, 4, 2, 2, 4, 8, 128), F32),
            vm((8, 32, 128), F32),
            vm((1, 128), F32),
            vm((4, 1, 128), F32),
            vm((4, 4, 1, 128), F32),
            vm((8, 4, 4, 1, 128), F32),
            vm((128, 128), F32),
            vm((128, 128), I32),
            vm((128, 128), F32),
            vm((12, 8, 768), F32),
            vm((8, 4, 128), F32),
            vm((8, 768, 128), BF16),
            vm((2, 2, 4, 2, 2, 8, 128), F32),
            vm((2, 2, 2, 4, 2, 2, 8, 128), F32),
            vm((2, 2, 4, 2, 2, 8, 128), F32),
            vm((2, 2, 4, 4, 8, 128), F32),
            vm((2, 2, 2, 4, 4, 8, 128), F32),
            vm((2, 2, 4, 4, 8, 128), F32),
            vm((4, 4, 2, 2, 8, 128), F32),
            vm((4, 4, 4, 8, 128), F32),
            vm((2, 2, 4, 8, 128), F32),
            vm((2, 2, 2, 4, 8, 128), F32),
            vm((2, 2, 4, 8, 128), F32),
            vm((2, 2, 4, 8, 128), F32),
            vm((2, 2, 2, 4, 8, 128), F32),
            vm((2, 2, 4, 8, 128), F32),
            vm((4, 2, 8, 4, 128), F32),
            vm((8, 8, 4, 128), F32),
            dma(()), dma(()), dma((14,)), dma((14,)),
            dma((6,)), dma((6,)), dma((6,)), dma((6,)), dma((6,)), dma((6,)), dma((6,)), dma((6,)),
            dma((4, 2)), dma((8,)), dma((2,)),
        ],
        compiler_params=pltpu.CompilerParams(collective_id=2, has_side_effects=True),
        name="finish",
    )(main, halo, row, sha, ref)


def per_device(raw_frames, gain_section, offset, gain_factor, row_map, column_map, reference_image, shifts):
    cal = calibrate(raw_frames.reshape(16, MR, MC), gain_section.reshape(16, MR // 8, MC), offset[0], gain_factor[0])
    image, rf, shc, sha = exchange(cal, reference_image, shifts.reshape(2, 64))
    row_mapped = jnp.dot(row_map, image, preferred_element_type=F32).astype(BF16)
    halves = swap(row_mapped)
    lab = jnp.dot(halves.reshape(IMG, IMG), column_map, preferred_element_type=F32).astype(BF16)
    core = (lax.axis_index("pulse") % 2).astype(I32).reshape(1)
    main, halo, row = track(core, shc, lab.reshape(2, 512, IMG), rf)
    new_reference, scores = finish(main, halo, row, sha, reference_image)
    return scores.reshape(1, 1, TILES), new_reference


def solution(mesh):
    return jax.shard_map(
        per_device,
        mesh=mesh,
        in_specs=(
            P("pulse", None, "mod", None, None),
            P("pulse", None, "mod", None, None),
            P("mod", None, None, None),
            P("mod", None, None, None),
            P(),
            P(),
            P(("mod", "pulse"), None),
            P(None, "pulse", "mod", None),
        ),
        out_specs=(P("pulse", "mod", None), P(("mod", "pulse"), None)),
        check_vma=False,
    )
```

```python
import jax
import jax.numpy as jnp
from jax import lax
from jax.experimental import pallas as pl
from jax.experimental.pallas import tpu as pltpu
from jax.sharding import PartitionSpec as P

MR = 128
MC = 512
TS = 128
SH = 24
TILES = 64
IMG = 1024
PRIOR = 16.0
MESH = pl.DeviceIdType.MESH
F32 = jnp.float32
BF16 = jnp.bfloat16
I32 = jnp.int32


def coords():
    mod = lax.axis_index("mod")
    pulse = lax.axis_index("pulse")
    z = mod // 2
    y = (pulse // 8) * 2 + mod % 2
    x = (pulse // 2) % 4
    core = pulse % 2
    return z, y, x, core


def device(z, y, x, core):
    return (z * 2 + y % 2, (y // 2) * 8 + x * 2 + core)


def remote(src, dst, send_sem, recv_sem, target):
    return pltpu.make_async_remote_copy(
        src_ref=src,
        dst_ref=dst,
        send_sem=send_sem,
        recv_sem=recv_sem,
        device_id=target,
        device_id_type=MESH,
    )


def greet(targets):
    barrier = pltpu.get_barrier_semaphore()
    for target in targets:
        pl.semaphore_signal(barrier, inc=1, device_id=target, device_id_type=MESH)
    pl.semaphore_wait(barrier, len(targets))


VM = pl.BlockSpec(memory_space=pltpu.VMEM)
ANY = pl.BlockSpec(memory_space=pl.ANY)


ORDER = (1, 7, 2, 6, 3, 5, 4)
SENDS = [(dz, 0) for dz in ORDER] + [(dz, 1) for dz in ORDER] + [(0, 1)]


def calibrate_frame(slot, raw, gain, off, fac, cal):
    k = lax.broadcasted_iota(I32, (8, MC), 0)
    inv = jnp.full((8, MC), 1.0, F32)
    for step in range(1, 8):
        inv = jnp.where(k == step, jnp.float32(1.0 / 3.0**step), inv)
    inv_next = inv * jnp.float32(1.0 / 3.0)

    def digits(row):
        packed = jnp.broadcast_to(gain[slot, pl.ds(row, 1), :].astype(F32) + 0.5, (8, MC))
        return jnp.floor(packed * inv) - 3.0 * jnp.floor(packed * inv_next)

    def step(p, carry):
        rows = pl.ds(pl.multiple_of(16 * p, 16), 16)
        digit = jnp.concatenate([digits(2 * p), digits(2 * p + 1)], axis=0)
        low = digit < 0.5
        mid = digit < 1.5
        dark = jnp.where(low, off[0, rows, :], jnp.where(mid, off[1, rows, :], off[2, rows, :]))
        scale = jnp.where(low, fac[0, rows, :], jnp.where(mid, fac[1, rows, :], fac[2, rows, :]))
        cal[slot, rows, :] = ((raw[slot, rows, :].astype(F32) - dark) * scale).astype(BF16)
        return carry

    lax.fori_loop(0, 8, step, 0)


def exchange_kernel(
    raw_hbm, gain_hbm, off_hbm, fac_hbm, rmap_hbm, cmap_hbm, ref_ref, sh_ref,
    lab_ref, rf_ref, shc_ref, sha_ref,
    raw, gain, off, fac, rmap, cmap, cal, img, acc, rm_own, rm_out, rm_in,
    ra, rtmp, rsl, rb, rc, srow, srow_in, sz, sy,
    in_sem, raw_sem, a_send, a_recv, r_send, r_recv, z_send, z_recv, y_send, y_recv,
    c_send, c_recv, x_send, x_recv, s_send, s_recv, m_send, m_recv, l_sem,
):
    z, y, x, core = coords()
    yl = y % 2
    mod = z * 2 + yl
    pulse = lax.axis_index("pulse")
    partner = device(z, y, x, 1 - core)

    def goal(dz, dl):
        return ((z + dz) % 8) * 2 + (yl + dl) % 2

    loads = [
        pltpu.make_async_copy(gain_hbm, gain, in_sem.at[0]),
        pltpu.make_async_copy(off_hbm, off, in_sem.at[1]),
        pltpu.make_async_copy(fac_hbm, fac, in_sem.at[2]),
    ]
    for copy in loads:
        copy.start()
    frames = SENDS + [(0, 0)]
    raw_loads = []
    for n, (dz, dl) in enumerate(frames):
        t = goal(dz, dl)
        copy = pltpu.make_async_copy(raw_hbm.at[t], raw.at[t], raw_sem.at[n])
        copy.start()
        raw_loads.append(copy)
    maps = [
        pltpu.make_async_copy(rmap_hbm, rmap, in_sem.at[3]),
        pltpu.make_async_copy(cmap_hbm, cmap, in_sem.at[4]),
    ]
    for copy in maps:
        copy.start()

    plane = [device(z, y, (x + (i // 2)) % 4, (core + i) % 2) for i in range(1, 8)]
    greet(
        [(goal(dz, dl), pulse) for dz, dl in SENDS]
        + plane
        + [device(z, (y + 2) % 4, x, core), device(z, (y + 3 - 2 * yl) % 4, x, core)]
    )

    j = x * 2 + core
    first = []
    for i in range(1, 8):
        copy = remote(ref_ref, ra.at[j], r_send.at[i - 1], r_recv.at[i - 1], plane[i - 1])
        copy.start()
        first.append(copy)
    own_ref = pltpu.make_async_copy(ref_ref, ra.at[j], l_sem.at[0])
    own_ref.start()

    lane = lax.broadcasted_iota(I32, (2, 128), 1)
    srow[:, 0:64] = sh_ref[...]
    srow[:, 64:128] = sh_ref[...]
    srow[...] = jnp.where(lane // 64 == core, srow[...], 0)
    s0 = remote(srow, srow_in, s_send.at[0], s_recv.at[0], partner)
    s0.start()

    for copy in loads:
        copy.wait()
    big = []

    def compute(n):
        raw_loads[n].wait()
        calibrate_frame(goal(*frames[n]), raw, gain, off, fac, cal)

    def send(n):
        t = goal(*SENDS[n])
        spot = img.at[z, pl.ds(pl.multiple_of(yl * MR, MR), MR)]
        copy = remote(cal.at[t], spot, a_send.at[n], a_recv.at[n], (t, pulse))
        copy.start()
        big.append(copy)

    compute(0)
    compute(1)

    for copy in first:
        copy.wait()
    own_ref.wait()
    mine = pl.ds(pl.multiple_of(j * 128, 128), 128)
    for i in range(8):
        rtmp[4 * i:4 * i + 4, :] = ra[i, :, mine].astype(F32)
    rsl[...] = rtmp[...].astype(BF16)
    second = []
    for i in range(1, 8):
        copy = remote(rsl, rb.at[z], z_send.at[i - 1], z_recv.at[i - 1], device((z + i) % 8, y, x, core))
        copy.start()
        second.append(copy)
    own_z = pltpu.make_async_copy(rsl, rb.at[z], l_sem.at[0])
    own_z.start()
    s0.wait()
    shc_ref[...] = srow[...] + srow_in[...]
    s1 = []
    for i in range(1, 8):
        copy = remote(shc_ref, sz.at[z], s_send.at[i], s_recv.at[i], device((z + i) % 8, y, x, core))
        copy.start()
        s1.append(copy)
    own_s = pltpu.make_async_copy(shc_ref, sz.at[z], l_sem.at[2])
    own_s.start()

    send(0)
    send(1)
    for n in range(2, 7):
        compute(n)
        send(n)

    for copy in second:
        copy.wait()
    own_z.wait()
    yrow = yl * 2 + y // 2
    third = []
    for i in range(1, 4):
        copy = remote(rb, rc.at[:, yrow], y_send.at[i - 1], y_recv.at[i - 1], device(z, (y + i) % 4, x, core))
        copy.start()
        third.append(copy)
    own_y = pltpu.make_async_copy(rb, rc.at[:, yrow], l_sem.at[0])
    own_y.start()
    for copy in s1:
        copy.wait()
    own_s.wait()
    s2 = []
    for i in range(1, 4):
        copy = remote(sz, sy.at[y], s_send.at[7 + i], s_recv.at[7 + i], device(z, (y + i) % 4, x, core))
        copy.start()
        s2.append(copy)
    own_s = pltpu.make_async_copy(sz, sy.at[y], l_sem.at[2])
    own_s.start()

    for n in range(7, 12):
        compute(n)
        send(n)

    for copy in third:
        copy.wait()
    own_y.wait()
    fourth = remote(rc.at[pl.ds(3 * (1 - core), 5)], rf_ref.at[x, core], c_send, c_recv, partner)
    fourth.start()
    own_c = pltpu.make_async_copy(rc.at[pl.ds(3 * core, 5)], rf_ref.at[x, core], l_sem.at[0])
    own_c.start()
    for copy in s2:
        copy.wait()
    own_s.wait()
    s3 = []
    for i in range(1, 4):
        copy = remote(sy, sha_ref.at[x], s_send.at[10 + i], s_recv.at[10 + i], device(z, y, (x + i) % 4, core))
        copy.start()
        s3.append(copy)
    own_s = pltpu.make_async_copy(sy, sha_ref.at[x], l_sem.at[2])
    own_s.start()

    for n in range(12, 15):
        compute(n)
        send(n)

    fourth.wait()
    own_c.wait()
    fifth = []
    for i in range(1, 4):
        copy = remote(rf_ref.at[x], rf_ref.at[x], x_send.at[i - 1], x_recv.at[i - 1], device(z, y, (x + i) % 4, core))
        copy.start()
        fifth.append(copy)

    compute(15)
    own = pltpu.make_async_copy(cal.at[mod], img.at[z, pl.ds(pl.multiple_of(yl * MR, MR), MR)], l_sem.at[1])
    own.start()
    acc[...] = jnp.zeros_like(acc)
    for copy in maps:
        copy.wait()
    own.wait()

    def add_rows(zz):
        half = (zz // 2) % 2
        k0 = pl.multiple_of((zz // 4) * 512 + (zz % 2) * 256, 256)

        def step(n, carry):
            cols = pl.ds(pl.multiple_of(n * 256, 256), 256)
            acc[half, :, cols] += jnp.dot(rmap[:, pl.ds(k0, 256)], img[zz, :, cols], preferred_element_type=F32)
            return carry

        lax.fori_loop(0, 2, step, 0)

    big[14].wait_recv()
    add_rows(z)
    for n in range(7):
        big[n].wait_recv()
        big[7 + n].wait_recv()
        add_rows((z + 8 - ORDER[n]) % 8)

    give = pl.ds(pl.multiple_of((1 - core) * 512, 512), 512)
    keep = pl.ds(pl.multiple_of(core * 512, 512), 512)
    for h in range(2):
        rm_out[:, 512 * h:512 * h + 512] = acc[h, give, :].astype(BF16)
    swap = remote(rm_out, rm_in, m_send, m_recv, partner)
    swap.start()
    for h in range(2):
        rm_own[:, 512 * h:512 * h + 512] = acc[h, keep, :].astype(BF16)

    def columns(source, g):
        def step(n, carry):
            cols = pl.ds(pl.multiple_of(n * 256, 256), 256)
            lab_ref[g, :, cols] = jnp.dot(source[...], cmap[:, cols], preferred_element_type=F32).astype(BF16)
            return carry

        lax.fori_loop(0, 4, step, 0)

    columns(rm_own, core)
    swap.wait()
    columns(rm_in, 1 - core)

    for copy in s3:
        copy.wait()
    own_s.wait()
    for copy in fifth:
        copy.wait()
    for copy in big:
        copy.wait_send()


def exchange(raw, gain, off, fac, rmap, cmap, ref, sh):
    dma = pltpu.SemaphoreType.DMA
    vm = pltpu.VMEM
    return pl.pallas_call(
        exchange_kernel,
        in_specs=[ANY, ANY, ANY, ANY, ANY, ANY, VM, VM],
        out_specs=[VM, VM, VM, VM],
        out_shape=[
            jax.ShapeDtypeStruct((2, 512, IMG), BF16),
            jax.ShapeDtypeStruct((4, 2, 5, 4, 32, 128), BF16),
            jax.ShapeDtypeStruct((2, 128), I32),
            jax.ShapeDtypeStruct((4, 4, 8, 2, 128), I32),
        ],
        scratch_shapes=[
            vm((16, MR, MC), BF16),
            vm((16, MR // 8, MC), I32),
            vm((3, MR, MC), F32),
            vm((3, MR, MC), F32),
            vm((IMG, IMG), BF16),
            vm((IMG, IMG), BF16),
            vm((16, MR, MC), BF16),
            vm((8, 256, 512), BF16),
            vm((2, IMG, 512), F32),
            vm((512, IMG), BF16),
            vm((512, IMG), BF16),
            vm((512, IMG), BF16),
            vm((8, 4, IMG), BF16),
            vm((32, 128), F32),
            vm((32, 128), BF16),
            vm((8, 32, 128), BF16),
            vm((8, 4, 32, 128), BF16),
            vm((2, 128), I32),
            vm((2, 128), I32),
            vm((8, 2, 128), I32),
            vm((4, 8, 2, 128), I32),
            dma((5,)), dma((16,)),
            dma((15,)), dma((15,)), dma((7,)), dma((7,)), dma((7,)), dma((7,)), dma((3,)), dma((3,)),
            dma(()), dma(()), dma((3,)), dma((3,)), dma((14,)), dma((14,)), dma(()), dma(()), dma((3,)),
        ],
        compiler_params=pltpu.CompilerParams(collective_id=0, has_side_effects=True),
        name="exchange",
    )(raw, gain, off, fac, rmap, cmap, ref, sh)


RROWS = 704
SROWS = 576


def track_kernel(core_ref, sh_ref, lab_ref, rf_ref, main_ref, halo_ref, row_ref, r3, held, part, wts, sp):
    core = core_ref[0]
    zero = jnp.zeros((RROWS, 128), F32)
    r3[0] = zero
    r3[9] = zero
    for b in range(8):
        r3[b + 1, 0:32, :] = jnp.zeros((32, 128), F32)
        r3[b + 1, 32:672, :] = rf_ref[b // 2, b % 2].reshape(640, 128).astype(F32)
        r3[b + 1, 672:704, :] = jnp.zeros((32, 128), F32)
    for b in range(10):
        sp[b] = jnp.zeros((SROWS, 128), F32)
    lane = lax.broadcasted_iota(I32, (TS, 128), 1)

    def place(t):
        g = t // 32
        ty = (t // 8) % 4
        tx = t % 8
        col = g * 64 + core * 32 + t % 32
        dy = sh_ref[0, col]
        dx = sh_ref[1, col]
        back = jnp.where(dx < 0, 1, 0).astype(I32)
        return g, ty, tx, dy, dx + 128 * back, tx + 1 - back

    def score_step(t, carry):
        g, ty, tx, dy, turn, block = place(t)
        tile = lab_ref[g, pl.ds(pl.multiple_of(ty * TS, TS), TS), pl.ds(pl.multiple_of(tx * 128, 128), 128)]
        tile = pltpu.roll(tile.astype(F32), turn, 1)
        held[t] = tile
        top = core * 128 + 32 + ty * TS + dy
        near = r3[block, pl.ds(top, TS), :]
        far = r3[block + 1, pl.ds(top, TS), :]
        product = tile * jnp.where(lane >= turn, near, far)
        part[t] = jnp.sum(product.reshape(16, 8, 128), axis=0)
        return carry

    lax.fori_loop(0, 64, score_step, 0)
    sums = jnp.sum(part[...], axis=1)
    score = jnp.broadcast_to(jnp.sum(sums, axis=1, keepdims=True) / TS, (64, 128))
    wts[...] = 1.0 / (1.0 + jnp.exp(-score))
    t_of = lax.broadcasted_iota(I32, (64, 128), 0)
    l_of = lax.broadcasted_iota(I32, (64, 128), 1)
    hit = l_of == (t_of // 32) * 64 + core * 32 + t_of % 32
    row_ref[...] = jnp.sum(jnp.where(hit, score, 0.0), axis=0, keepdims=True)

    def splat_step(t, carry):
        g, ty, tx, dy, turn, block = place(t)
        value = held[t] * wts[pl.ds(t, 1), :]
        top = 32 + ty * TS + dy
        sp[block, pl.ds(top, TS), :] += jnp.where(lane >= turn, value, 0.0)
        sp[block + 1, pl.ds(top, TS), :] += jnp.where(lane >= turn, 0.0, value)
        return carry

    lax.fori_loop(0, 64, splat_step, 0)
    edge = pl.multiple_of((1 - core) * 544, 32)
    for b in range(8):
        main_ref[b] = sp[b + 1, 32:544, :]
        halo_ref[b] = sp[b + 1, pl.ds(edge, 32), :]


def track(core, shc, lab, rf):
    return pl.pallas_call(
        track_kernel,
        in_specs=[
            pl.BlockSpec(memory_space=pltpu.SMEM),
            pl.BlockSpec(memory_space=pltpu.SMEM),
            VM,
            VM,
        ],
        out_specs=[VM, VM, VM],
        out_shape=[
            jax.ShapeDtypeStruct((8, 512, 128), F32),
            jax.ShapeDtypeStruct((8, 32, 128), F32),
            jax.ShapeDtypeStruct((1, 128), F32),
        ],
        scratch_shapes=[
            pltpu.VMEM((10, RROWS, 128), F32),
            pltpu.VMEM((64, TS, 128), F32),
            pltpu.VMEM((64, 8, 128), F32),
            pltpu.VMEM((64, 128), F32),
            pltpu.VMEM((10, SROWS, 128), F32),
        ],
        name="track",
    )(core, shc, lab, rf)


def ring_start(piece, me, right, left, fwd_a, fwd_b, fin_l, fin_r, send, recv):
    copies = [
        remote(piece((me + 2) % 4, 0), fwd_a, send.at[0], recv.at[0], right),
        remote(piece((me + 2) % 4, 1), fwd_b, send.at[1], recv.at[1], left),
        remote(piece((me + 1) % 4, 1), fin_l.at[1], send.at[2], recv.at[2], right),
        remote(piece((me + 3) % 4, 0), fin_r.at[0], send.at[3], recv.at[3], left),
    ]
    for copy in copies:
        copy.start()
    return copies


def ring_pass(piece, me, right, left, fwd_a, fwd_b, fin_l, fin_r, sum_a, sum_b, send, recv, copies):
    copies[0].wait_recv()
    sum_a[...] = fwd_a[...] + piece((me + 1) % 4, 0)[...]
    onward_a = remote(sum_a, fin_l.at[0], send.at[4], recv.at[4], right)
    onward_a.start()
    copies[1].wait_recv()
    sum_b[...] = fwd_b[...] + piece((me + 3) % 4, 1)[...]
    onward_b = remote(sum_b, fin_r.at[1], send.at[5], recv.at[5], left)
    onward_b.start()
    return copies + [onward_a, onward_b]


def ring_end(copies):
    for n, copy in enumerate(copies):
        copy.wait_send()
        if n >= 2:
            copy.wait_recv()


def finish_kernel(
    main_ref, halo_ref, row_ref, sha_ref, ref_ref,
    out_ref, score_ref,
    acc, halo_in, row_in, wr, wx, wy, wz, smat, dmat, wmat, lhs, cov, unit, p_fwd, p_fin, p_sum, q_fwd, q_fin, q_sum, mid_p, mid_q,
    p2_fwd, p2_fin, p2_sum, q2_fwd, q2_fin, q2_sum, zout, zin,
    h_send, h_recv, w_send, w_recv, p_send, p_recv, q_send, q_recv, p2_send, p2_recv, q2_send, q2_recv,
    z_send, z_recv, l_sem,
):
    z, y, x, core = coords()
    partner = device(z, y, x, 1 - core)
    xs = [device(z, y, (x + i) % 4, core) for i in range(1, 4)]
    ys = [device(z, (y + i) % 4, x, core) for i in range(1, 4)]
    zs = [device((z + i) % 8, y, x, core) for i in range(1, 8)]
    zo = [device((z + i) % 8, y, x, 1 - core) for i in range(1, 8)]
    greet([partner] + xs + ys + zs + zo)

    halo = remote(halo_ref, halo_in, h_send, h_recv, partner)
    halo.start()
    row = remote(row_ref, row_in, w_send.at[0], w_recv.at[0], partner)
    row.start()
    acc[...] = main_ref[...].reshape(acc.shape)
    halo.wait()
    edge = 3 - 3 * core
    yl = 1 - core
    for b in range(8):
        acc[b, edge, yl, yl] += halo_in[b].reshape(4, 8, 128)

    def piece_px(d, half):
        return acc.at[pl.ds(2 * half, 2), :, :, :, d]

    def piece_qy(d, half):
        return acc.at[pl.ds(4 + 2 * half, 2), :, d % 2, d // 2]

    xr, xl = xs[0], xs[2]
    yr, yl_dev = ys[0], ys[2]
    args_p = (piece_px, x, xr, xl, p_fwd.at[0], p_fwd.at[1], p_fin.at[0], p_fin.at[1])
    args_q = (piece_qy, y, yr, yl_dev, q_fwd.at[0], q_fwd.at[1], q_fin.at[0], q_fin.at[1])
    cp = ring_start(*args_p, p_send, p_recv)
    cq = ring_start(*args_q, q_send, q_recv)

    row.wait()
    chip = row_ref[...] + row_in[...]
    both = jnp.where(core == 0, chip[:, 0:64], chip[:, 64:128])
    score_ref[...] = both
    wr[...] = chip
    w1 = []
    for i in range(7):
        copy = remote(wr, wx.at[z], w_send.at[1 + i], w_recv.at[1 + i], zs[i])
        copy.start()
        w1.append(copy)
    own_w = pltpu.make_async_copy(wr, wx.at[z], l_sem.at[0])
    own_w.start()

    cp = ring_pass(*args_p, p_sum.at[0], p_sum.at[1], p_send, p_recv, cp)
    cq = ring_pass(*args_q, q_sum.at[0], q_sum.at[1], q_send, q_recv, cq)

    for copy in w1:
        copy.wait()
    own_w.wait()
    w2 = []
    for i in range(3):
        copy = remote(wx, wy.at[y], w_send.at[8 + i], w_recv.at[8 + i], ys[i])
        copy.start()
        w2.append(copy)
    own_w = pltpu.make_async_copy(wx, wy.at[y], l_sem.at[0])
    own_w.start()

    gather_rows(sha_ref, 0, smat, 8)
    gather_rows(sha_ref, 1, dmat, 8)
    smat[...] = jnp.transpose(smat[...])
    lane = lax.broadcasted_iota(I32, (128, 128), 1)
    for k in range(3):
        ty = jnp.clip(z - 1 + k, 0, 7)
        for g in range(2):
            moved = pltpu.roll(dmat[...], (128 - (g * 64 + ty * 8)) % 128, 1)
            for tx in range(8):
                dx = jnp.broadcast_to(moved[:, tx:tx + 1], (128, 128))
                edge_hit = jnp.where(lane < 64, jnp.where(lane < dx, 1.0, 0.0), jnp.where(lane >= 128 + dx, 1.0, 0.0))
                edge_hit = jnp.where(lane == 63, 1.0, edge_hit)
                unit[tx, pl.ds((2 * k + g) * 128, 128), :] = edge_hit.astype(BF16)

    for copy in w2:
        copy.wait()
    own_w.wait()
    w3 = []
    for i in range(3):
        copy = remote(wy, wz.at[x], w_send.at[11 + i], w_recv.at[11 + i], xs[i])
        copy.start()
        w3.append(copy)
    own_w2 = pltpu.make_async_copy(wy, wz.at[x], l_sem.at[0])
    own_w2.start()

    ring_end(cp)
    for h in range(2):
        mid_p[pl.ds(2 * h, 2)] = piece_px(x, h)[...] + p_fin[0, h] + p_fin[1, h]

    def piece_py(d, half):
        return mid_p.at[pl.ds(2 * half, 2), :, d % 2, d // 2]

    args_p2 = (piece_py, y, yr, yl_dev, p2_fwd.at[0], p2_fwd.at[1], p2_fin.at[0], p2_fin.at[1])
    cp2 = ring_start(*args_p2, p2_send, p2_recv)
    ring_end(cq)
    for h in range(2):
        mid_q[pl.ds(2 * h, 2)] = piece_qy(y, h)[...] + q_fin[0, h] + q_fin[1, h]

    def piece_qx(d, half):
        return mid_q.at[pl.ds(2 * half, 2), :, d]

    args_q2 = (piece_qx, x, xr, xl, q2_fwd.at[0], q2_fwd.at[1], q2_fin.at[0], q2_fin.at[1])
    cq2 = ring_start(*args_q2, q2_send, q2_recv)
    cp2 = ring_pass(*args_p2, p2_sum.at[0], p2_sum.at[1], p2_send, p2_recv, cp2)
    cq2 = ring_pass(*args_q2, q2_sum.at[0], q2_sum.at[1], q2_send, q2_recv, cq2)
    ring_end(cp2)
    ring_end(cq2)
    for h in range(2):
        got_p = piece_py(y, h)[...] + p2_fin[0, h] + p2_fin[1, h]
        got_q = piece_qx(x, h)[...] + q2_fin[0, h] + q2_fin[1, h]
        for b in range(2):
            for d in range(4):
                zout[d, 0, 2 * h + b] = got_p[b, d, 0:4, :]
                zout[d, 1, 2 * h + b] = got_p[b, d, 4:8, :]
                zout[d, 0, 4 + 2 * h + b] = got_q[b, d, 0:4, :]
                zout[d, 1, 4 + 2 * h + b] = got_q[b, d, 4:8, :]

    for d in range(4):
        for c in range(2):
            target_z = 4 * core + d
            self_hit = jnp.logical_and(target_z == z, core == c)

            @pl.when(jnp.logical_not(self_hit))
            def _():
                remote(zout.at[d, c], zin.at[z], z_send.at[d, c], z_recv.at[z], device(target_z, y, x, c)).start()

            @pl.when(self_hit)
            def _():
                pltpu.make_async_copy(zout.at[d, c], zin.at[z], l_sem.at[1]).start()

    for copy in w3:
        copy.wait()
    own_w2.wait()
    gather_rows(wz, 0, wmat, 8)
    wmat[...] = jnp.transpose(1.0 / (1.0 + jnp.exp(-wmat[...])))
    r0 = z * 128 + (y % 2) * 64 + (y // 2) * 32 + x * 8 + core * 4
    for k in range(3):
        ty = jnp.clip(z - 1 + k, 0, 7)
        valid = jnp.where(ty == z - 1 + k, 1.0, 0.0).astype(F32)
        for g in range(2):
            rows = pl.ds(pl.multiple_of(g * 64 + ty * 8, 8), 8)
            low = smat[rows, :] + (ty * 128).astype(F32)
            w = wmat[rows, :] * valid
            w1 = w.astype(BF16).astype(F32)
            w2 = (w - w1).astype(BF16).astype(F32)
            w3 = w - w1 - w2
            cols = slice((2 * k + g) * 128, (2 * k + g + 1) * 128)
            for i in range(4):
                r = (r0 + i).astype(F32)
                hit = jnp.logical_and(low <= r, r < low + 128.0)
                for n, part in enumerate((w1, w2, w3)):
                    lhs[n * 4 + i, :, cols] = jnp.where(hit, part, 0.0)
    left = lhs[...].reshape(96, 768).astype(BF16)
    sub = lax.broadcasted_iota(I32, (12, 8, 128), 1)
    found = jnp.zeros((12, 8, 128), F32)
    for tx in range(8):
        product = jnp.dot(left, unit[tx], preferred_element_type=F32).reshape(12, 8, 128)
        found = jnp.where(sub == tx, product, found)
    found = found[0:4] + found[4:8] + found[8:12]
    tx_of = lax.broadcasted_iota(I32, (8, 128), 0)
    l_of = lax.broadcasted_iota(I32, (8, 128), 1)
    for i in range(4):
        total = jnp.sum(jnp.where(l_of == 63, found[i], 0.0), axis=1, keepdims=True)
        side = jnp.where(l_of == 63, 0.0, found[i])
        before = jnp.where(tx_of == 0, 0.0, pltpu.roll(side, 1, 0))
        after = jnp.where(tx_of == 7, 0.0, pltpu.roll(side, 7, 0))
        cover = total - side + jnp.where(l_of < 64, before, after)
        for b in range(8):
            cov[b, i:i + 1, :] = cover[b:b + 1, :]

    for d in range(4):
        for c in range(2):
            target_z = 4 * core + d
            self_hit = jnp.logical_and(target_z == z, core == c)

            @pl.when(jnp.logical_not(self_hit))
            def _():
                remote(zout.at[d, c], zin.at[z], z_send.at[d, c], z_recv.at[z], device(target_z, y, x, c)).wait_send()

    for s in range(8):
        self_hit = jnp.logical_and(z == s, core == z // 4)

        @pl.when(jnp.logical_not(self_hit))
        def _():
            remote(zout.at[0, 0], zin.at[s], z_send.at[0, 0], z_recv.at[s], partner).wait_recv()

        @pl.when(self_hit)
        def _():
            pltpu.make_async_copy(zout.at[0, 0], zin.at[s], l_sem.at[1]).wait()

    own_ref = ref_ref[...].astype(F32)
    for b in range(8):
        total = zin[0, b]
        for s in range(1, 8):
            total = total + zin[s, b]
        cols = slice(128 * b, 128 * b + 128)
        out_ref[:, cols] = (total + PRIOR * own_ref[:, cols]) / (cov[b] + PRIOR)


def gather_rows(source, which, target, inner):
    def step(i, carry):
        row = source[i // (4 * inner), (i // inner) % 4, i % inner, which:which + 1, :]
        target[pl.ds(i, 1), :] = row.astype(target.dtype)
        return carry

    lax.fori_loop(0, 128, step, 0)


def finish(main, halo, row, sha, ref):
    dma = pltpu.SemaphoreType.DMA
    vm = pltpu.VMEM
    return pl.pallas_call(
        finish_kernel,
        in_specs=[VM, VM, VM, VM, VM],
        out_specs=[VM, VM],
        out_shape=[
            jax.ShapeDtypeStruct((4, IMG), F32),
            jax.ShapeDtypeStruct((1, 64), F32),
        ],
        scratch_shapes=[
            vm((8, 4, 2, 2, 4, 8, 128), F32),
            vm((8, 32, 128), F32),
            vm((1, 128), F32),
            vm((1, 128), F32),
            vm((8, 1, 128), F32),
            vm((4, 8, 1, 128), F32),
            vm((4, 4, 8, 1, 128), F32),
            vm((128, 128), F32),
            vm((128, 128), I32),
            vm((128, 128), F32),
            vm((12, 8, 768), F32),
            vm((8, 4, 128), F32),
            vm((8, 768, 128), BF16),
            vm((2, 2, 4, 2, 2, 8, 128), F32),
            vm((2, 2, 2, 4, 2, 2, 8, 128), F32),
            vm((2, 2, 4, 2, 2, 8, 128), F32),
            vm((2, 2, 4, 4, 8, 128), F32),
            vm((2, 2, 2, 4, 4, 8, 128), F32),
            vm((2, 2, 4, 4, 8, 128), F32),
            vm((4, 4, 2, 2, 8, 128), F32),
            vm((4, 4, 4, 8, 128), F32),
            vm((2, 2, 4, 8, 128), F32),
            vm((2, 2, 2, 4, 8, 128), F32),
            vm((2, 2, 4, 8, 128), F32),
            vm((2, 2, 4, 8, 128), F32),
            vm((2, 2, 2, 4, 8, 128), F32),
            vm((2, 2, 4, 8, 128), F32),
            vm((4, 2, 8, 4, 128), F32),
            vm((8, 8, 4, 128), F32),
            dma(()), dma(()), dma((14,)), dma((14,)),
            dma((6,)), dma((6,)), dma((6,)), dma((6,)), dma((6,)), dma((6,)), dma((6,)), dma((6,)),
            dma((4, 2)), dma((8,)), dma((2,)),
        ],
        compiler_params=pltpu.CompilerParams(collective_id=2, has_side_effects=True),
        name="finish",
    )(main, halo, row, sha, ref)


def per_device(raw_frames, gain_section, offset, gain_factor, row_map, column_map, reference_image, shifts):
    lab, rf, shc, sha = exchange(
        raw_frames.reshape(16, MR, MC),
        gain_section.reshape(16, MR // 8, MC),
        offset[0],
        gain_factor[0],
        row_map,
        column_map,
        reference_image,
        shifts.reshape(2, 64),
    )
    core = (lax.axis_index("pulse") % 2).astype(I32).reshape(1)
    main, halo, row = track(core, shc, lab, rf)
    new_reference, scores = finish(main, halo, row, sha, reference_image)
    return scores.reshape(1, 1, TILES), new_reference


def solution(mesh):
    return jax.shard_map(
        per_device,
        mesh=mesh,
        in_specs=(
            P("pulse", None, "mod", None, None),
            P("pulse", None, "mod", None, None),
            P("mod", None, None, None),
            P("mod", None, None, None),
            P(),
            P(),
            P(("mod", "pulse"), None),
            P(None, "pulse", "mod", None),
        ),
        out_specs=(P("pulse", "mod", None), P(("mod", "pulse"), None)),
        check_vma=False,
    )
```
